128 devices in a mesh: pts: 16 (over z, y), hrs: 8 (over x, core).
Axes of the slice: x: 4, y: 4, z: 4, core: 2. Of those that a mesh axis runs over, the one named last changes fastest.
Arguments:
- fields: float32 [512, 262144], P(('pts', 'hrs')), may hold values from -2000 to 2000, as said below
- probes: float32 [256, 512], replicated, may hold values from -0.25 to 0.25
Outputs:
- basis_rows: float32 [256, 262144], P(None, ('pts', 'hrs'))
- coeffs: float32 [256, 512], replicated
The draws below stay inside these ranges and needn't reach their ends.
Inputs may be any that keep to these rules, and one draw needn't show every extreme that they name: `fields`: every hour and every grid point carries its own scale, and the values are real-valued and never all zero.
All inputs are finite; a program needn't handle non-finite values.
Results may differ from the reference program's by a relative error of at most 0.00017.
Values sent between devices are 32-bit elements; how exact they have to be, the bound alone decides.
No kernel may reach another device: no remote copies, remote signals or barrier semaphores. Data moves between devices by JAX's collectives and lax.ppermute only.
A program may use at most 64 MiB of HBM per device.

```python
import jax
import jax.numpy as jnp
from jax import lax

K = 256
HOURS = 512
POINTS = 262144


def draw_fields(key, part):
    keys_all = jax.random.split(jax.random.fold_in(key, 11), 3)
    point_scale = 10.0 ** jax.random.uniform(keys_all[1], (1, POINTS), dtype=jnp.float32)
    lat_ramp = 1.0 + 2.0 * jnp.arange(POINTS, dtype=jnp.float32)[None, :] / (POINTS - 1)
    hour_scale = 10.0 ** jax.random.uniform(keys_all[0], (HOURS, 1), dtype=jnp.float32)
    noise_part = jnp.clip(jax.random.normal(keys_all[2], (HOURS, POINTS), dtype=jnp.float32), -4.0, 4.0)
    return hour_scale * point_scale * lat_ramp * noise_part


def gaussian(own_key, extent, width, most, held_as=jnp.bfloat16):
    values = width * jax.random.normal(own_key, extent, jnp.float32)
    return jnp.clip(values, min=-most, max=most).astype(held_as)


def setup_inputs(seed: int = 0) -> dict:
    key_of = jax.random.split(jax.random.key(seed), 3)
    fields = draw_fields(jax.random.fold_in(key_of[2], 71), 0)
    probes = gaussian(key_of[1], (K, HOURS), HOURS ** -0.5, 0.25, jnp.float32)
    return {"fields": fields, "probes": probes}


highest = lax.Precision.HIGHEST

def reference(fields, probes):
    n_points = fields.shape[1]
    sketched = jnp.dot(probes.astype(jnp.float32), fields.astype(jnp.float32), precision=highest, preferred_element_type=jnp.float32)
    gram = lax.dot_general(sketched.astype(jnp.float32), sketched.astype(jnp.float32), (((1,), (1,)), ((), ())), precision=highest, preferred_element_type=jnp.float32) / n_points
    lower = jnp.linalg.cholesky(gram)
    basis_rows = lax.linalg.triangular_solve(lower, sketched, left_side=True, lower=True)
    coeffs = lax.dot_general(basis_rows.astype(jnp.float32), fields.astype(jnp.float32), (((1,), (1,)), ((), ())), precision=highest, preferred_element_type=jnp.float32) / n_points
    return (basis_rows, coeffs)
```

```python
import jax
import jax.numpy as jnp
from jax import lax
from jax.experimental import pallas as pl
from jax.experimental.pallas import tpu as pltpu
from jax.sharding import PartitionSpec as P

highest = lax.Precision.HIGHEST
AXES = ("pts", "hrs")
BLOCK = 64


def dot_nn(left, right):
    return jnp.dot(left, right, precision=highest, preferred_element_type=jnp.float32)


def dot_tn(left, right):
    return lax.dot_general(
        left, right, (((0,), (0,)), ((), ())), precision=highest, preferred_element_type=jnp.float32
    )


def dot_nt(left, right):
    return lax.dot_general(
        left, right, (((1,), (1,)), ((), ())), precision=highest, preferred_element_type=jnp.float32
    )


def sketch_body(scale, fields_ref, probes_ref, sketched_ref, moment_ref):
    step = pl.program_id(0)
    devs, per, pts = fields_ref.shape
    hours = devs * per
    panel = fields_ref[...].reshape(hours, pts)
    sketched = dot_nn(probes_ref[...], panel)
    sketched_ref[...] = sketched
    moment = (dot_nt(sketched, panel) * scale).reshape(-1, 8, hours)

    @pl.when(step == 0)
    def _():
        for c in range(hours // 128):
            moment_ref[:, c] = moment[:, :, 128 * c : 128 * c + 128]

    @pl.when(step > 0)
    def _():
        for c in range(hours // 128):
            moment_ref[:, c] += moment[:, :, 128 * c : 128 * c + 128]


def sketch(panels, probes, scale, width=1024):
    devs, per, pts = panels.shape
    k, hours = probes.shape
    width = min(width, pts)
    return pl.pallas_call(
        lambda *refs: sketch_body(scale, *refs),
        name="sketch",
        grid=(pts // width,),
        in_specs=[
            pl.BlockSpec((devs, per, width), lambda i: (0, 0, i)),
            pl.BlockSpec((k, hours), lambda i: (0, 0)),
        ],
        out_specs=[
            pl.BlockSpec((k, width), lambda i: (0, i)),
            pl.BlockSpec((k // 8, hours // 128, 8, 128), lambda i: (0, 0, 0, 0)),
        ],
        out_shape=[
            jax.ShapeDtypeStruct((k, pts), jnp.float32),
            jax.ShapeDtypeStruct((k // 8, hours // 128, 8, 128), jnp.float32),
        ],
        compiler_params=pltpu.CompilerParams(vmem_limit_bytes=48 << 20),
    )(panels, probes)


def inverse_factor(block, left):
    n, lanes = block.shape
    row = lax.broadcasted_iota(jnp.int32, (n, lanes), 0)
    lane = lax.broadcasted_iota(jnp.int32, (n, lanes), 1)
    off = 0 if left else n
    for j in range(n):
        pivot = block[j : j + 1, off + j : off + j + 1]
        column = jnp.broadcast_to(block[:, off + j : off + j + 1], (n, lanes))
        block = block - jnp.where(row > j, column, 0.0) * (block[j : j + 1, :] * (1.0 / pivot))
    pivots = jnp.sum(jnp.where(lane == row + off, block, 0.0), axis=1, keepdims=True)
    block = block * lax.rsqrt(pivots)
    return block[:, n:] if left else block[:, :n]


def factor_body(moment_ref, probes_ref, sketched_ref, basis_ref, coeffs_ref, work_ref):
    tiles = moment_ref.shape[1]
    k = sketched_ref.shape[0]
    moment = jnp.concatenate([moment_ref[:, c].reshape(k, 128) for c in range(tiles)], axis=1)
    row = lax.broadcasted_iota(jnp.int32, (k, k), 0)
    col = lax.broadcasted_iota(jnp.int32, (k, k), 1)
    work_ref[:, :k] = dot_nt(moment, probes_ref[...])
    work_ref[:, k:] = jnp.where(row == col, 1.0, 0.0)
    n = BLOCK
    brow = lax.broadcasted_iota(jnp.int32, (n, 2 * n), 0)
    blane = lax.broadcasted_iota(jnp.int32, (n, 2 * n), 1)
    for b in range(k // n):
        lo = n * b
        left = b % 2 == 0
        lane0 = 2 * n * (b // 2)
        block = work_ref[lo : lo + n, lane0 : lane0 + 2 * n]
        if left:
            block = jnp.where(blane < n, block, jnp.where(blane - n == brow, 1.0, 0.0))
        else:
            block = jnp.where(blane >= n, block, jnp.where(blane == brow, 1.0, 0.0))
        upper = dot_nn(inverse_factor(block, left), work_ref[lo : lo + n, :])
        work_ref[lo : lo + n, k:] = upper[:, k:]
        if lo + n < k:
            update = dot_tn(upper[:, :k], upper)
            work_ref[lo + n :, :] = work_ref[lo + n :, :] - update[lo + n :, :]
    inverse = work_ref[:, k:]
    basis_ref[...] = dot_nn(inverse, sketched_ref[...])
    coeffs_ref[...] = dot_nn(inverse, moment)


def factor_and_apply(moment, probes, sketched):
    k, pts = sketched.shape
    return pl.pallas_call(
        factor_body,
        name="factor_and_apply",
        out_shape=[
            jax.ShapeDtypeStruct((k, pts), jnp.float32),
            jax.ShapeDtypeStruct(probes.shape, jnp.float32),
        ],
        scratch_shapes=[pltpu.VMEM((k, 2 * k), jnp.float32)],
        compiler_params=pltpu.CompilerParams(vmem_limit_bytes=48 << 20),
    )(moment, probes, sketched)


def on_device(fields, probes):
    devices = lax.axis_size("pts") * lax.axis_size("hrs")
    per, n_points = fields.shape
    sent = fields.reshape(per, devices, n_points // devices).transpose(1, 0, 2)
    panels = lax.all_to_all(sent, AXES, split_axis=0, concat_axis=0, tiled=True)
    sketched, moment = sketch(panels, probes, 1.0 / n_points)
    parts = moment.reshape(devices, -1, 128)
    parts = lax.all_to_all(parts, AXES, split_axis=0, concat_axis=0, tiled=True)
    total = jnp.broadcast_to(jnp.sum(parts, axis=0)[None], parts.shape)
    total = lax.all_to_all(total, AXES, split_axis=0, concat_axis=0, tiled=True)
    basis_rows, coeffs = factor_and_apply(total.reshape(moment.shape), probes, sketched)
    return (basis_rows, coeffs)


def solution(mesh):
    return jax.shard_map(
        on_device,
        mesh=mesh,
        in_specs=(P(AXES, None), P()),
        out_specs=(P(None, AXES), P()),
        check_vma=False,
    )
```

```python
import jax
import jax.numpy as jnp
from jax import lax
from jax.experimental import pallas as pl
from jax.experimental.pallas import tpu as pltpu
from jax.sharding import PartitionSpec as P

highest = lax.Precision.HIGHEST
AXES = ("pts", "hrs")
BLOCK = 64


def dot_nn(left, right):
    return jnp.dot(left, right, precision=highest, preferred_element_type=jnp.float32)


def dot_tn(left, right):
    return lax.dot_general(
        left, right, (((0,), (0,)), ((), ())), precision=highest, preferred_element_type=jnp.float32
    )


def dot_nt(left, right):
    return lax.dot_general(
        left, right, (((1,), (1,)), ((), ())), precision=highest, preferred_element_type=jnp.float32
    )


def sketch_body(scale, fields_ref, probes_ref, sketched_ref, moment_ref):
    step = pl.program_id(0)
    devs, per, pts = fields_ref.shape
    hours = devs * per
    panel = fields_ref[...].reshape(hours, pts)
    sketched = dot_nn(probes_ref[...], panel)
    sketched_ref[...] = sketched
    moment = (dot_nt(sketched, panel) * scale).reshape(-1, 8, hours)

    @pl.when(step == 0)
    def _():
        for c in range(hours // 128):
            moment_ref[:, c] = moment[:, :, 128 * c : 128 * c + 128]

    @pl.when(step > 0)
    def _():
        for c in range(hours // 128):
            moment_ref[:, c] += moment[:, :, 128 * c : 128 * c + 128]


def sketch(panels, probes, scale, width=1024):
    devs, per, pts = panels.shape
    k, hours = probes.shape
    width = min(width, pts)
    return pl.pallas_call(
        lambda *refs: sketch_body(scale, *refs),
        name="sketch",
        grid=(pts // width,),
        in_specs=[
            pl.BlockSpec((devs, per, width), lambda i: (0, 0, i)),
            pl.BlockSpec((k, hours), lambda i: (0, 0)),
        ],
        out_specs=[
            pl.BlockSpec((k, width), lambda i: (0, i)),
            pl.BlockSpec((k // 8, hours // 128, 8, 128), lambda i: (0, 0, 0, 0)),
        ],
        out_shape=[
            jax.ShapeDtypeStruct((k, pts), jnp.float32),
            jax.ShapeDtypeStruct((k // 8, hours // 128, 8, 128), jnp.float32),
        ],
        compiler_params=pltpu.CompilerParams(vmem_limit_bytes=48 << 20),
    )(panels, probes)


def spread(x):
    return jnp.broadcast_to(x, (8, 128))


def inverse_factor(block, left):
    n = block.shape[0]
    off = 0 if left else n
    sublane = lax.broadcasted_iota(jnp.int32, (8, 128), 0)
    tiles = [block[8 * v : 8 * v + 8, :] for v in range(n // 8)]
    done = []
    for t in range(n // 8):
        cols = {}
        for v in range(t, n // 8):
            for i in range(8):
                lane = off + 8 * t + i
                cols[v, i] = spread(tiles[v][:, lane : lane + 1])
        rows = [spread(tiles[t][i : i + 1, :]) for i in range(8)]
        inverses = []
        pivots = None
        for i in range(8):
            pivot = spread(cols[t, i][i : i + 1, :])
            pivots = pivot if i == 0 else jnp.where(sublane == i, pivot, pivots)
            inverses.append(1.0 / pivot)
            for j in range(i + 1, 8):
                ratio = inverses[i] * spread(cols[t, j][i : i + 1, :])
                for v in range(t, n // 8):
                    cols[v, j] = cols[v, j] - cols[v, i] * ratio
                rows[j] = rows[j] - ratio * rows[i]
        for v in range(t + 1, n // 8):
            for i in range(8):
                tiles[v] = tiles[v] - (cols[v, i] * inverses[i]) * rows[i]
        tile = rows[0]
        for i in range(1, 8):
            tile = jnp.where(sublane == i, rows[i], tile)
        done.append(tile * lax.rsqrt(pivots))
    block = jnp.concatenate(done, axis=0)
    return block[:, n:] if left else block[:, :n]


def factor_body(moment_ref, probes_ref, sketched_ref, basis_ref, coeffs_ref, work_ref):
    tiles = moment_ref.shape[1]
    k = sketched_ref.shape[0]
    moment = jnp.concatenate([moment_ref[:, c].reshape(k, 128) for c in range(tiles)], axis=1)
    row = lax.broadcasted_iota(jnp.int32, (k, k), 0)
    col = lax.broadcasted_iota(jnp.int32, (k, k), 1)
    work_ref[:, :k] = dot_nt(moment, probes_ref[...])
    work_ref[:, k:] = jnp.where(row == col, 1.0, 0.0)
    n = BLOCK
    brow = lax.broadcasted_iota(jnp.int32, (n, 2 * n), 0)
    blane = lax.broadcasted_iota(jnp.int32, (n, 2 * n), 1)
    for b in range(k // n):
        lo = n * b
        left = b % 2 == 0
        lane0 = 2 * n * (b // 2)
        block = work_ref[lo : lo + n, lane0 : lane0 + 2 * n]
        if left:
            block = jnp.where(blane < n, block, jnp.where(blane - n == brow, 1.0, 0.0))
        else:
            block = jnp.where(blane >= n, block, jnp.where(blane == brow, 1.0, 0.0))
        upper = dot_nn(inverse_factor(block, left), work_ref[lo : lo + n, :])
        work_ref[lo : lo + n, k:] = upper[:, k:]
        if lo + n < k:
            update = dot_tn(upper[:, :k], upper)
            work_ref[lo + n :, :] = work_ref[lo + n :, :] - update[lo + n :, :]
    inverse = work_ref[:, k:]
    basis_ref[...] = dot_nn(inverse, sketched_ref[...])
    coeffs_ref[...] = dot_nn(inverse, moment)


def factor_and_apply(moment, probes, sketched):
    k, pts = sketched.shape
    return pl.pallas_call(
        factor_body,
        name="factor_and_apply",
        out_shape=[
            jax.ShapeDtypeStruct((k, pts), jnp.float32),
            jax.ShapeDtypeStruct(probes.shape, jnp.float32),
        ],
        scratch_shapes=[pltpu.VMEM((k, 2 * k), jnp.float32)],
        compiler_params=pltpu.CompilerParams(vmem_limit_bytes=48 << 20),
    )(moment, probes, sketched)


def on_device(fields, probes):
    devices = lax.axis_size("pts") * lax.axis_size("hrs")
    per, n_points = fields.shape
    sent = fields.reshape(per, devices, n_points // devices).transpose(1, 0, 2)
    panels = lax.all_to_all(sent, AXES, split_axis=0, concat_axis=0, tiled=True)
    sketched, moment = sketch(panels, probes, 1.0 / n_points)
    parts = moment.reshape(devices, -1, 128)
    parts = lax.all_to_all(parts, AXES, split_axis=0, concat_axis=0, tiled=True)
    total = jnp.broadcast_to(jnp.sum(parts, axis=0)[None], parts.shape)
    total = lax.all_to_all(total, AXES, split_axis=0, concat_axis=0, tiled=True)
    basis_rows, coeffs = factor_and_apply(total.reshape(moment.shape), probes, sketched)
    return (basis_rows, coeffs)


def solution(mesh):
    return jax.shard_map(
        on_device,
        mesh=mesh,
        in_specs=(P(AXES, None), P()),
        out_specs=(P(None, AXES), P()),
        check_vma=False,
    )
```

```python
import jax
import jax.numpy as jnp
from jax import lax
from jax.experimental import pallas as pl
from jax.experimental.pallas import tpu as pltpu
from jax.sharding import PartitionSpec as P

highest = lax.Precision.HIGHEST
AXES = ("pts", "hrs")
CHUNK = 512
HALF = 128
BLOCK = 32
PANEL = 16


def dot_nn(left, right):
    return jnp.dot(left, right, precision=highest, preferred_element_type=jnp.float32)


def dot_tn(left, right):
    return lax.dot_general(
        left, right, (((0,), (0,)), ((), ())), precision=highest, preferred_element_type=jnp.float32
    )


def dot_nt(left, right):
    return lax.dot_general(
        left, right, (((1,), (1,)), ((), ())), precision=highest, preferred_element_type=jnp.float32
    )


def split(x):
    high = x.astype(jnp.bfloat16)
    return high, (x - high.astype(jnp.float32)).astype(jnp.bfloat16)


def dot_split(left, right_high, right_low):
    high, low = split(left)
    return jnp.dot(
        jnp.concatenate([high, high, low], axis=1),
        jnp.concatenate([right_high, right_low, right_high], axis=0),
        preferred_element_type=jnp.float32,
    )


def sketch_body(scale, panels_ref, probes_ref, high_ref, low_ref, moment_ref, raw_ref, fields_high, fields_low, sems):
    count, devs, per, width = raw_ref.shape
    hours = devs * per
    copies = [
        pltpu.make_async_copy(panels_ref.at[:, :, width * c : width * c + width], raw_ref.at[c], sems.at[c])
        for c in range(count)
    ]
    for copy in copies:
        copy.start()
    probes = probes_ref[...]
    for c in range(count):
        copies[c].wait()
        cols = slice(width * c, width * c + width)
        high, low = split(raw_ref[c].reshape(hours, width))
        fields_high[:, cols] = high
        fields_low[:, cols] = low
        high_ref[:, cols], low_ref[:, cols] = split(dot_split(probes, high, low))
    high, low = high_ref[...], low_ref[...]
    moment = lax.dot_general(
        jnp.concatenate([high, high, low], axis=1),
        jnp.concatenate([fields_high[...], fields_low[...], fields_high[...]], axis=1),
        (((1,), (1,)), ((), ())),
        preferred_element_type=jnp.float32,
    )
    moment = (moment * scale).reshape(-1, 8, hours)
    for c in range(hours // 128):
        moment_ref[:, c] = moment[:, :, 128 * c : 128 * c + 128]


def sketch(panels, probes, scale):
    devs, per, pts = panels.shape
    k, hours = probes.shape
    width = min(CHUNK, pts)
    count = pts // width
    vmem = pl.BlockSpec(memory_space=pltpu.VMEM)
    return pl.pallas_call(
        lambda *refs: sketch_body(scale, *refs),
        name="sketch",
        in_specs=[pl.BlockSpec(memory_space=pl.ANY), vmem],
        out_specs=[vmem, vmem, vmem],
        out_shape=[
            jax.ShapeDtypeStruct((k, pts), jnp.bfloat16),
            jax.ShapeDtypeStruct((k, pts), jnp.bfloat16),
            jax.ShapeDtypeStruct((k // 8, hours // 128, 8, 128), jnp.float32),
        ],
        scratch_shapes=[
            pltpu.VMEM((count, devs, per, width), jnp.float32),
            pltpu.VMEM((hours, pts), jnp.bfloat16),
            pltpu.VMEM((hours, pts), jnp.bfloat16),
            pltpu.SemaphoreType.DMA((count,)),
        ],
        compiler_params=pltpu.CompilerParams(vmem_limit_bytes=48 << 20),
    )(panels, probes)


def spread(x):
    return jnp.broadcast_to(x, (8, 128))


def eliminate(tiles, offset):
    sublane = lax.broadcasted_iota(jnp.int32, (8, 128), 0)
    lane = lax.broadcasted_iota(jnp.int32, (8, 128), 1)
    tiles = list(tiles)
    count = len(tiles)
    done = []
    for t in range(0, count, PANEL // 8):
        first = offset + 8 * t
        own = (lane >= first) & (lane < first + PANEL)
        cols = {}
        for v in range(t, count):
            for i in range(PANEL):
                cols[v, i] = spread(tiles[v][:, first + i : first + i + 1])
        rows = []
        for u in range(PANEL // 8):
            unit = jnp.where(lane - first - 8 * u == sublane, 1.0, 0.0)
            tile = jnp.where(own, unit, tiles[t + u])
            rows += [spread(tile[i : i + 1, :]) for i in range(8)]
        inverses = []
        pivots = []
        for i in range(PANEL):
            v0, s = t + i // 8, i % 8
            pivots.append(spread(cols[v0, i][s : s + 1, :]))
            inverses.append(1.0 / pivots[i])
            for j in range(i + 1, PANEL):
                ratio = inverses[i] * spread(cols[v0, j][s : s + 1, :])
                for v in range(v0, count):
                    cols[v, j] = cols[v, j] - cols[v, i] * ratio
                rows[j] = rows[j] - ratio * rows[i]
        for v in range(t + PANEL // 8, count):
            tiles[v] = jnp.where(own, 0.0, tiles[v])
            for i in range(PANEL):
                tiles[v] = tiles[v] - (cols[v, i] * inverses[i]) * rows[i]
        for u in range(PANEL // 8):
            tile, pivot = rows[8 * u], pivots[8 * u]
            for i in range(1, 8):
                tile = jnp.where(sublane == i, rows[8 * u + i], tile)
                pivot = jnp.where(sublane == i, pivots[8 * u + i], pivot)
            done.append(tile * lax.rsqrt(pivot))
    return done


def inverse_factor(matrix):
    n = matrix.shape[0]
    row = lax.broadcasted_iota(jnp.int32, (n, n), 0)
    lane = lax.broadcasted_iota(jnp.int32, (n, n), 1)
    tiles = [matrix[8 * v : 8 * v + 8] for v in range(n // 8)]
    per = BLOCK // 8
    for b in range(n // BLOCK):
        lo = BLOCK * b
        here = slice(per * b, per * b + per)
        tiles[here] = eliminate(tiles[here], lo)
        if lo + BLOCK < n:
            block = jnp.concatenate(tiles[here], axis=0)
            above = (lane[:BLOCK] > row[:BLOCK] + lo) & (lane[:BLOCK] < lo + BLOCK)
            update = dot_tn(block, jnp.where(above, 0.0, block))
            own = (lane[:8] >= lo) & (lane[:8] < lo + BLOCK)
            for v in range(per * b + per, n // 8):
                tiles[v] = jnp.where(own, 0.0, tiles[v]) - update[8 * v : 8 * v + 8]
    return jnp.where(lane <= row, jnp.concatenate(tiles, axis=0), 0.0)


def factor_body(moment_ref, probes_ref, high_ref, low_ref, basis_ref, coeffs_ref, out_ref, sems):
    n = HALF
    k = high_ref.shape[0]
    moment = jnp.concatenate([moment_ref[:, c].reshape(k, 128) for c in range(moment_ref.shape[1])], axis=1)
    probes = probes_ref[...]
    moment_high, moment_low = split(moment)

    def apply(part, inverse):
        rows = pl.ds(part * n, n)
        used = inverse.shape[1]
        out_ref[rows, :] = dot_split(inverse, high_ref[:used, :], low_ref[:used, :])
        copy = pltpu.make_async_copy(out_ref.at[rows, :], basis_ref.at[rows, :], sems.at[part])
        copy.start()
        coeffs_ref[rows, :] = dot_split(inverse, moment_high[:used], moment_low[:used])
        return copy

    upper = inverse_factor(dot_nt(moment[:n], probes[:n]))
    cross = dot_nn(upper, dot_nt(moment[:n], probes[n:]))
    lower = inverse_factor(dot_nt(moment[n:], probes[n:]) - dot_tn(cross, cross))
    first = apply(0, upper)
    corner = dot_nn(lower, dot_tn(cross, upper))
    second = apply(1, jnp.concatenate([-corner, lower], axis=1))
    first.wait()
    second.wait()


def factor_and_apply(moment, probes, high, low):
    k, pts = high.shape
    vmem = pl.BlockSpec(memory_space=pltpu.VMEM)
    return pl.pallas_call(
        factor_body,
        name="factor_and_apply",
        in_specs=[vmem, vmem, vmem, vmem],
        out_specs=[pl.BlockSpec(memory_space=pl.ANY), vmem],
        out_shape=[
            jax.ShapeDtypeStruct((k, pts), jnp.float32),
            jax.ShapeDtypeStruct(probes.shape, jnp.float32),
        ],
        scratch_shapes=[pltpu.VMEM((k, pts), jnp.float32), pltpu.SemaphoreType.DMA((2,))],
        compiler_params=pltpu.CompilerParams(vmem_limit_bytes=48 << 20),
    )(moment, probes, high, low)


def on_device(fields, probes):
    devices = lax.axis_size("pts") * lax.axis_size("hrs")
    per, n_points = fields.shape
    sent = fields.reshape(per, devices, n_points // devices).transpose(1, 0, 2)
    panels = lax.all_to_all(sent, AXES, split_axis=0, concat_axis=0, tiled=True)
    high, low, moment = sketch(panels, probes, 1.0 / n_points)
    parts = moment.reshape(devices, -1, 128)
    parts = lax.all_to_all(parts, AXES, split_axis=0, concat_axis=0, tiled=True)
    total = jnp.broadcast_to(jnp.sum(parts, axis=0)[None], parts.shape)
    total = lax.all_to_all(total, AXES, split_axis=0, concat_axis=0, tiled=True)
    basis_rows, coeffs = factor_and_apply(total.reshape(moment.shape), probes, high, low)
    return (basis_rows, coeffs)


def solution(mesh):
    return jax.shard_map(
        on_device,
        mesh=mesh,
        in_specs=(P(AXES, None), P()),
        out_specs=(P(None, AXES), P()),
        check_vma=False,
    )
```

```python
import jax
import jax.numpy as jnp
from jax import lax
from jax.experimental import pallas as pl
from jax.experimental.pallas import tpu as pltpu
from jax.sharding import PartitionSpec as P

highest = lax.Precision.HIGHEST
AXES = ("pts", "hrs")
CHUNK = 512
HALF = 128
BLOCK = 32
PANEL = 16


def dot_nn(left, right):
    return jnp.dot(left, right, precision=highest, preferred_element_type=jnp.float32)


def dot_tn(left, right):
    return lax.dot_general(
        left, right, (((0,), (0,)), ((), ())), precision=highest, preferred_element_type=jnp.float32
    )


def dot_nt(left, right):
    return lax.dot_general(
        left, right, (((1,), (1,)), ((), ())), precision=highest, preferred_element_type=jnp.float32
    )


def split(x):
    high = x.astype(jnp.bfloat16)
    return high, (x - high.astype(jnp.float32)).astype(jnp.bfloat16)


def dot_split(left, right_high, right_low):
    high, low = split(left)
    return jnp.dot(
        jnp.concatenate([high, high, low], axis=1),
        jnp.concatenate([right_high, right_low, right_high], axis=0),
        preferred_element_type=jnp.float32,
    )


def sketch_body(scale, panels_ref, probes_ref, high_ref, low_ref, moment_ref, fields_high, fields_low):
    devs, per, pts = panels_ref.shape
    hours = devs * per
    width = min(CHUNK, pts)
    probes = probes_ref[...]
    for c in range(pts // width):
        cols = slice(width * c, width * c + width)
        high, low = split(panels_ref[:, :, cols].reshape(hours, width))
        fields_high[:, cols] = high
        fields_low[:, cols] = low
        high_ref[:, cols], low_ref[:, cols] = split(dot_split(probes, high, low))
    high, low = high_ref[...], low_ref[...]
    moment = lax.dot_general(
        jnp.concatenate([high, high, low], axis=1),
        jnp.concatenate([fields_high[...], fields_low[...], fields_high[...]], axis=1),
        (((1,), (1,)), ((), ())),
        preferred_element_type=jnp.float32,
    )
    moment = (moment * scale).reshape(-1, 8, hours)
    for c in range(hours // 128):
        moment_ref[:, c] = moment[:, :, 128 * c : 128 * c + 128]


def sketch(panels, probes, scale):
    devs, per, pts = panels.shape
    k, hours = probes.shape
    vmem = pl.BlockSpec(memory_space=pltpu.VMEM)
    return pl.pallas_call(
        lambda *refs: sketch_body(scale, *refs),
        name="sketch",
        in_specs=[vmem, vmem],
        out_specs=[vmem, vmem, vmem],
        out_shape=[
            jax.ShapeDtypeStruct((k, pts), jnp.bfloat16),
            jax.ShapeDtypeStruct((k, pts), jnp.bfloat16),
            jax.ShapeDtypeStruct((k // 8, hours // 128, 8, 128), jnp.float32),
        ],
        scratch_shapes=[
            pltpu.VMEM((hours, pts), jnp.bfloat16),
            pltpu.VMEM((hours, pts), jnp.bfloat16),
        ],
        compiler_params=pltpu.CompilerParams(vmem_limit_bytes=32 << 20),
    )(panels, probes)


def spread(x):
    return jnp.broadcast_to(x, (8, 128))


def eliminate(tiles, offset):
    sublane = lax.broadcasted_iota(jnp.int32, (8, 128), 0)
    lane = lax.broadcasted_iota(jnp.int32, (8, 128), 1)
    tiles = list(tiles)
    count = len(tiles)
    for t in range(0, count, PANEL // 8):
        first = offset + 8 * t
        own = (lane >= first) & (lane < first + PANEL)
        cols = {}
        for i in range(PANEL):
            for v in range(t + i // 8, count):
                cols[v, i] = spread(tiles[v][:, first + i : first + i + 1])
        for v in range(t, count):
            tiles[v] = jnp.where(own, jnp.where(lane - first - 8 * (v - t) == sublane, 1.0, 0.0), tiles[v])
        for i in range(PANEL):
            top, s = t + i // 8, i % 8
            pivot = spread(cols[top, i][s : s + 1, :])
            pivots = pivot if s == 0 else jnp.where(sublane == s, pivot, pivots)
            inverse = 1.0 / pivot
            scaled = {v: cols[v, i] * inverse for v in range(top, count)}
            for j in range(i + 1, PANEL):
                u, r = t + j // 8, j % 8
                if j == i + 1:
                    ratio = inverse * spread(cols[u, i][r : r + 1, :])
                else:
                    ratio = spread(scaled[u][r : r + 1, :])
                for v in range(u, count):
                    cols[v, j] = cols[v, j] - cols[v, i] * ratio
            row = spread(tiles[top][s : s + 1, :])
            if s < 7:
                tiles[top] = tiles[top] - jnp.where(sublane > s, scaled[top], 0.0) * row
            for v in range(top + 1, count):
                tiles[v] = tiles[v] - scaled[v] * row
            if s == 7:
                tiles[top] = tiles[top] * lax.rsqrt(pivots)
    return tiles


def inverse_factor(matrix):
    n = matrix.shape[0]
    row = lax.broadcasted_iota(jnp.int32, (n, n), 0)
    lane = lax.broadcasted_iota(jnp.int32, (n, n), 1)
    tiles = [matrix[8 * v : 8 * v + 8] for v in range(n // 8)]
    per = BLOCK // 8
    for b in range(n // BLOCK):
        lo = BLOCK * b
        here = slice(per * b, per * b + per)
        tiles[here] = eliminate(tiles[here], lo)
        if lo + BLOCK < n:
            block = jnp.concatenate(tiles[here], axis=0)
            above = (lane[:BLOCK] > row[:BLOCK] + lo) & (lane[:BLOCK] < lo + BLOCK)
            update = dot_tn(block, jnp.where(above, 0.0, block))
            own = (lane[:8] >= lo) & (lane[:8] < lo + BLOCK)
            for v in range(per * b + per, n // 8):
                tiles[v] = jnp.where(own, 0.0, tiles[v]) - update[8 * v : 8 * v + 8]
    return jnp.where(lane <= row, jnp.concatenate(tiles, axis=0), 0.0)


def factor_body(moment_ref, probes_ref, high_ref, low_ref, basis_ref, coeffs_ref, out_ref, sems):
    n = HALF
    k, pts = high_ref.shape
    moment = jnp.concatenate([moment_ref[:, c].reshape(k, 128) for c in range(moment_ref.shape[1])], axis=1)
    probes = probes_ref[...]
    copies = []

    def write(rows, cols, values):
        where = (pl.ds(rows, values.shape[0]), pl.ds(cols, values.shape[1]))
        out_ref[where] = values
        copies.append(pltpu.make_async_copy(out_ref.at[where], basis_ref.at[where], sems.at[len(copies)]))
        copies[-1].start()

    upper = inverse_factor(dot_nt(moment[:n], probes[:n]))
    cross = dot_nn(upper, dot_nt(moment[:n], probes[n:]))
    rest = dot_nt(moment[n:], probes[n:]) - dot_tn(cross, cross)
    basis = dot_split(upper, high_ref[:n, :], low_ref[:n, :])
    write(0, 0, basis)
    coeffs = dot_split(upper, *split(moment[:n]))
    coeffs_ref[:n, :] = coeffs
    second = high_ref[n:, :].astype(jnp.float32) + low_ref[n:, :].astype(jnp.float32)
    high, low = split(second - dot_split(cross.T, *split(basis)))
    moment_high, moment_low = split(moment[n:] - dot_split(cross.T, *split(coeffs)))
    lower = inverse_factor(rest)
    coeffs_ref[n:, :] = dot_split(lower, moment_high, moment_low)
    for c in range(0, pts, pts // 2):
        cols = slice(c, c + pts // 2)
        write(n, c, dot_split(lower, high[:, cols], low[:, cols]))
    for copy in copies:
        copy.wait()


def factor_and_apply(moment, probes, high, low):
    k, pts = high.shape
    vmem = pl.BlockSpec(memory_space=pltpu.VMEM)
    return pl.pallas_call(
        factor_body,
        name="factor_and_apply",
        in_specs=[vmem, vmem, vmem, vmem],
        out_specs=[pl.BlockSpec(memory_space=pl.ANY), vmem],
        out_shape=[
            jax.ShapeDtypeStruct((k, pts), jnp.float32),
            jax.ShapeDtypeStruct(probes.shape, jnp.float32),
        ],
        scratch_shapes=[pltpu.VMEM((k, pts), jnp.float32), pltpu.SemaphoreType.DMA((3,))],
        compiler_params=pltpu.CompilerParams(vmem_limit_bytes=32 << 20),
    )(moment, probes, high, low)


def on_device(fields, probes):
    devices = lax.axis_size("pts") * lax.axis_size("hrs")
    per, n_points = fields.shape
    sent = fields.reshape(per, devices, n_points // devices).transpose(1, 0, 2)
    panels = lax.all_to_all(sent, AXES, split_axis=0, concat_axis=0, tiled=True)
    high, low, moment = sketch(panels, probes, 1.0 / n_points)
    parts = moment.reshape(devices, -1, 128)
    parts = lax.all_to_all(parts, AXES, split_axis=0, concat_axis=0, tiled=True)
    total = jnp.broadcast_to(jnp.sum(parts, axis=0)[None], parts.shape)
    total = lax.all_to_all(total, AXES, split_axis=0, concat_axis=0, tiled=True)
    basis_rows, coeffs = factor_and_apply(total.reshape(moment.shape), probes, high, low)
    return (basis_rows, coeffs)


def solution(mesh):
    return jax.shard_map(
        on_device,
        mesh=mesh,
        in_specs=(P(AXES, None), P()),
        out_specs=(P(None, AXES), P()),
        check_vma=False,
    )
```

```python
import jax
import jax.numpy as jnp
from jax import lax
from jax.experimental import pallas as pl
from jax.experimental.pallas import tpu as pltpu
from jax.sharding import PartitionSpec as P

highest = lax.Precision.HIGHEST
AXES = ("pts", "hrs")
CHUNK = 512
HALF = 128
BLOCK = 32
PANEL = 16


def dot_nn(left, right):
    return jnp.dot(left, right, precision=highest, preferred_element_type=jnp.float32)


def dot_tn(left, right):
    return lax.dot_general(
        left, right, (((0,), (0,)), ((), ())), precision=highest, preferred_element_type=jnp.float32
    )


def dot_nt(left, right):
    return lax.dot_general(
        left, right, (((1,), (1,)), ((), ())), precision=highest, preferred_element_type=jnp.float32
    )


def split(x):
    high = x.astype(jnp.bfloat16)
    return high, (x - high.astype(jnp.float32)).astype(jnp.bfloat16)


def dot_split(left, right_high, right_low):
    high, low = split(left)
    return jnp.dot(
        jnp.concatenate([high, high, low], axis=1),
        jnp.concatenate([right_high, right_low, right_high], axis=0),
        preferred_element_type=jnp.float32,
    )


def sketch_body(scale, panels_ref, probes_ref, high_ref, low_ref, moment_ref, fields_high, fields_low):
    devs, per, pts = panels_ref.shape
    hours = devs * per
    width = min(CHUNK, pts)
    probes = probes_ref[...]
    for c in range(pts // width):
        cols = slice(width * c, width * c + width)
        high, low = split(panels_ref[:, :, cols].reshape(hours, width))
        fields_high[:, cols] = high
        fields_low[:, cols] = low
        high_ref[:, cols], low_ref[:, cols] = split(dot_split(probes, high, low))
    high, low = high_ref[...], low_ref[...]
    moment = lax.dot_general(
        jnp.concatenate([high, high, low], axis=1),
        jnp.concatenate([fields_high[...], fields_low[...], fields_high[...]], axis=1),
        (((1,), (1,)), ((), ())),
        preferred_element_type=jnp.float32,
    )
    moment = (moment * scale).reshape(-1, 8, hours)
    for c in range(hours // 128):
        moment_ref[:, c] = moment[:, :, 128 * c : 128 * c + 128]


def sketch(panels, probes, scale):
    devs, per, pts = panels.shape
    k, hours = probes.shape
    vmem = pl.BlockSpec(memory_space=pltpu.VMEM)
    return pl.pallas_call(
        lambda *refs: sketch_body(scale, *refs),
        name="sketch",
        in_specs=[vmem, vmem],
        out_specs=[vmem, vmem, vmem],
        out_shape=[
            jax.ShapeDtypeStruct((k, pts), jnp.bfloat16),
            jax.ShapeDtypeStruct((k, pts), jnp.bfloat16),
            jax.ShapeDtypeStruct((k // 8, hours // 128, 8, 128), jnp.float32),
        ],
        scratch_shapes=[
            pltpu.VMEM((hours, pts), jnp.bfloat16),
            pltpu.VMEM((hours, pts), jnp.bfloat16),
        ],
        compiler_params=pltpu.CompilerParams(vmem_limit_bytes=32 << 20),
    )(panels, probes)


def spread(x):
    return jnp.broadcast_to(x, (8, 128))


def eliminate(tiles, offset):
    sublane = lax.broadcasted_iota(jnp.int32, (8, 128), 0)
    lane = lax.broadcasted_iota(jnp.int32, (8, 128), 1)
    tiles = list(tiles)
    count = len(tiles)
    for t in range(0, count, PANEL // 8):
        first = offset + 8 * t
        own = (lane >= first) & (lane < first + PANEL)
        cols = {}
        for i in range(PANEL):
            for v in range(t + i // 8, count):
                cols[v, i] = spread(tiles[v][:, first + i : first + i + 1])
        for v in range(t, count):
            tiles[v] = jnp.where(own, jnp.where(lane - first - 8 * (v - t) == sublane, 1.0, 0.0), tiles[v])
        pivot = spread(cols[t, 0][0:1, :])
        for i in range(PANEL):
            top, s = t + i // 8, i % 8
            pivots = pivot if s == 0 else jnp.where(sublane == s, pivot, pivots)
            inverse = 1.0 / pivot
            scaled = {v: cols[v, i] * inverse for v in range(top, count)}
            if i + 1 < PANEL:
                u, r = t + (i + 1) // 8, (i + 1) % 8
                below = spread(cols[u, i][r : r + 1, :])
                pivot = spread(cols[u, i + 1][r : r + 1, :]) - (below * below) * inverse
            for j in range(i + 1, PANEL):
                u, r = t + j // 8, j % 8
                ratio = inverse * below if j == i + 1 else spread(scaled[u][r : r + 1, :])
                for v in range(u, count):
                    cols[v, j] = cols[v, j] - cols[v, i] * ratio
            row = spread(tiles[top][s : s + 1, :])
            if s < 7:
                tiles[top] = tiles[top] - jnp.where(sublane > s, scaled[top], 0.0) * row
            for v in range(top + 1, count):
                tiles[v] = tiles[v] - scaled[v] * row
            if s == 7:
                tiles[top] = tiles[top] * lax.rsqrt(pivots)
    return tiles


def inverse_factor(matrix):
    n = matrix.shape[0]
    row = lax.broadcasted_iota(jnp.int32, (n, n), 0)
    lane = lax.broadcasted_iota(jnp.int32, (n, n), 1)
    tiles = [matrix[8 * v : 8 * v + 8] for v in range(n // 8)]
    per = BLOCK // 8
    for b in range(n // BLOCK):
        lo = BLOCK * b
        here = slice(per * b, per * b + per)
        tiles[here] = eliminate(tiles[here], lo)
        if lo + BLOCK < n:
            block = jnp.concatenate(tiles[here], axis=0)
            above = (lane[:BLOCK] > row[:BLOCK] + lo) & (lane[:BLOCK] < lo + BLOCK)
            update = dot_tn(block, jnp.where(above, 0.0, block))
            own = (lane[:8] >= lo) & (lane[:8] < lo + BLOCK)
            for v in range(per * b + per, n // 8):
                tiles[v] = jnp.where(own, 0.0, tiles[v]) - update[8 * v : 8 * v + 8]
    return jnp.where(lane <= row, jnp.concatenate(tiles, axis=0), 0.0)


def factor_body(moment_ref, probes_ref, high_ref, low_ref, basis_ref, coeffs_ref, basis_out, coeffs_out, sems):
    n = HALF
    k, pts = high_ref.shape
    moment = jnp.concatenate([moment_ref[:, c].reshape(k, 128) for c in range(moment_ref.shape[1])], axis=1)
    probes = probes_ref[...]
    copies = []

    def write(held, ref, rows, cols, values):
        where = (pl.ds(rows, values.shape[0]), pl.ds(cols, values.shape[1]))
        held[where] = values
        copies.append(pltpu.make_async_copy(held.at[where], ref.at[where], sems.at[len(copies)]))
        copies[-1].start()

    upper = inverse_factor(dot_nt(moment[:n], probes[:n]))
    cross = dot_nn(upper, dot_nt(moment[:n], probes[n:]))
    rest = dot_nt(moment[n:], probes[n:]) - dot_tn(cross, cross)
    basis = dot_split(upper, high_ref[:n, :], low_ref[:n, :])
    write(basis_out, basis_ref, 0, 0, basis)
    coeffs = dot_split(upper, *split(moment[:n]))
    write(coeffs_out, coeffs_ref, 0, 0, coeffs)
    second = high_ref[n:, :].astype(jnp.float32) + low_ref[n:, :].astype(jnp.float32)
    high, low = split(second - dot_split(cross.T, *split(basis)))
    moment_high, moment_low = split(moment[n:] - dot_split(cross.T, *split(coeffs)))
    lower = inverse_factor(rest)
    for c in range(0, pts, pts // 2):
        cols = slice(c, c + pts // 2)
        write(basis_out, basis_ref, n, c, dot_split(lower, high[:, cols], low[:, cols]))
    write(coeffs_out, coeffs_ref, n, 0, dot_split(lower, moment_high, moment_low))
    for copy in copies:
        copy.wait()


def factor_and_apply(moment, probes, high, low):
    k, pts = high.shape
    vmem = pl.BlockSpec(memory_space=pltpu.VMEM)
    return pl.pallas_call(
        factor_body,
        name="factor_and_apply",
        in_specs=[vmem, vmem, vmem, vmem],
        out_specs=[pl.BlockSpec(memory_space=pl.ANY), pl.BlockSpec(memory_space=pl.ANY)],
        out_shape=[
            jax.ShapeDtypeStruct((k, pts), jnp.float32),
            jax.ShapeDtypeStruct(probes.shape, jnp.float32),
        ],
        scratch_shapes=[
            pltpu.VMEM((k, pts), jnp.float32),
            pltpu.VMEM(probes.shape, jnp.float32),
            pltpu.SemaphoreType.DMA((5,)),
        ],
        compiler_params=pltpu.CompilerParams(vmem_limit_bytes=32 << 20),
    )(moment, probes, high, low)


def on_device(fields, probes):
    devices = lax.axis_size("pts") * lax.axis_size("hrs")
    per, n_points = fields.shape
    sent = fields.reshape(per, devices, n_points // devices).transpose(1, 0, 2)
    panels = lax.all_to_all(sent, AXES, split_axis=0, concat_axis=0, tiled=True)
    high, low, moment = sketch(panels, probes, 1.0 / n_points)
    parts = moment.reshape(devices, -1, 128)
    parts = lax.all_to_all(parts, AXES, split_axis=0, concat_axis=0, tiled=True)
    total = jnp.broadcast_to(jnp.sum(parts, axis=0)[None], parts.shape)
    total = lax.all_to_all(total, AXES, split_axis=0, concat_axis=0, tiled=True)
    basis_rows, coeffs = factor_and_apply(total.reshape(moment.shape), probes, high, low)
    return (basis_rows, coeffs)


def solution(mesh):
    return jax.shard_map(
        on_device,
        mesh=mesh,
        in_specs=(P(AXES, None), P()),
        out_specs=(P(None, AXES), P()),
        check_vma=False,
    )
```

```python
import jax
import jax.numpy as jnp
from jax import lax
from jax.experimental import pallas as pl
from jax.experimental.pallas import tpu as pltpu
from jax.sharding import Mesh
from jax.sharding import PartitionSpec as P

highest = lax.Precision.HIGHEST
CHIPS = ("pts", "chip")
AXES = ("pts", "chip", "core")
SWAP = ((0, 1), (1, 0))
CHUNK = 512
HALF = 128
BLOCK = 32
PANEL = 16


def dot_nn(left, right):
    return jnp.dot(left, right, precision=highest, preferred_element_type=jnp.float32)


def dot_tn(left, right):
    return lax.dot_general(
        left, right, (((0,), (0,)), ((), ())), precision=highest, preferred_element_type=jnp.float32
    )


def dot_nt(left, right):
    return lax.dot_general(
        left, right, (((1,), (1,)), ((), ())), precision=highest, preferred_element_type=jnp.float32
    )


def split(x):
    high = x.astype(jnp.bfloat16)
    return high, (x - high.astype(jnp.float32)).astype(jnp.bfloat16)


def dot_split(left, right_high, right_low):
    high, low = split(left)
    return jnp.dot(
        jnp.concatenate([high, high, low], axis=1),
        jnp.concatenate([right_high, right_low, right_high], axis=0),
        preferred_element_type=jnp.float32,
    )


def moment_half(scale, half, high_ref, low_ref, fields_high, fields_low, moment_ref):
    hours = fields_high.shape[0] // 2
    rows = pl.ds(pl.multiple_of(half * hours, hours), hours)
    high = fields_high[rows, :]
    moment = lax.dot_general(
        jnp.concatenate([high_ref[...], high_ref[...], low_ref[...]], axis=1),
        jnp.concatenate([high, fields_low[rows, :], high], axis=1),
        (((1,), (1,)), ((), ())),
        preferred_element_type=jnp.float32,
    )
    moment = (moment * scale).reshape(-1, 8, hours)
    for c in range(hours // 128):
        moment_ref[:, c] = moment[:, :, 128 * c : 128 * c + 128]


def sketch_body(scale, panels_ref, probes_ref, high_ref, low_ref, fields_high, fields_low, moment_ref):
    devs, per, pts = panels_ref.shape
    hours = devs * per
    width = min(CHUNK, pts)
    probes = probes_ref[...]
    for c in range(pts // width):
        cols = slice(width * c, width * c + width)
        high, low = split(panels_ref[:, :, cols].reshape(hours, width))
        fields_high[:, cols] = high
        fields_low[:, cols] = low
        high_ref[:, cols], low_ref[:, cols] = split(dot_split(probes, high, low))
    moment_half(scale, 1 - lax.axis_index("core"), high_ref, low_ref, fields_high, fields_low, moment_ref)


def own_body(scale, high_ref, low_ref, fields_high, fields_low, moment_ref):
    moment_half(scale, lax.axis_index("core"), high_ref, low_ref, fields_high, fields_low, moment_ref)


def sketch(panels, probes, scale):
    devs, per, pts = panels.shape
    k, hours = probes.shape
    vmem = pl.BlockSpec(memory_space=pltpu.VMEM)
    params = pltpu.CompilerParams(vmem_limit_bytes=32 << 20)
    moment = jax.ShapeDtypeStruct((k // 8, hours // 256, 8, 128), jnp.float32)
    parts = [jax.ShapeDtypeStruct((n, pts), jnp.bfloat16) for n in (k, k, hours, hours)]
    *held, other = pl.pallas_call(
        lambda *refs: sketch_body(scale, *refs),
        name="sketch",
        in_specs=[vmem, vmem],
        out_specs=[vmem] * 5,
        out_shape=[*parts, moment],
        compiler_params=params,
    )(panels, probes)
    own = pl.pallas_call(
        lambda *refs: own_body(scale, *refs),
        name="own_moment",
        in_specs=[vmem] * 4,
        out_specs=vmem,
        out_shape=moment,
        compiler_params=params,
    )(*held)
    return held[0], held[1], own, other


def spread(x):
    return jnp.broadcast_to(x, (8, 128))


def eliminate(tiles, offset):
    sublane = lax.broadcasted_iota(jnp.int32, (8, 128), 0)
    lane = lax.broadcasted_iota(jnp.int32, (8, 128), 1)
    tiles = list(tiles)
    count = len(tiles)
    for t in range(0, count, PANEL // 8):
        first = offset + 8 * t
        own = (lane >= first) & (lane < first + PANEL)
        cols = {}
        for i in range(PANEL):
            for v in range(t + i // 8, count):
                cols[v, i] = spread(tiles[v][:, first + i : first + i + 1])
        for v in range(t, count):
            tiles[v] = jnp.where(own, jnp.where(lane - first - 8 * (v - t) == sublane, 1.0, 0.0), tiles[v])
        pivot = spread(cols[t, 0][0:1, :])
        for i in range(PANEL):
            top, s = t + i // 8, i % 8
            pivots = pivot if s == 0 else jnp.where(sublane == s, pivot, pivots)
            inverse = 1.0 / pivot
            scaled = {v: cols[v, i] * inverse for v in range(top, count)}
            if i + 1 < PANEL:
                u, r = t + (i + 1) // 8, (i + 1) % 8
                below = spread(cols[u, i][r : r + 1, :])
                pivot = spread(cols[u, i + 1][r : r + 1, :]) - (below * below) * inverse
            for j in range(i + 1, PANEL):
                u, r = t + j // 8, j % 8
                ratio = inverse * below if j == i + 1 else spread(scaled[u][r : r + 1, :])
                for v in range(u, count):
                    cols[v, j] = cols[v, j] - cols[v, i] * ratio
            row = spread(tiles[top][s : s + 1, :])
            if s < 7:
                tiles[top] = tiles[top] - jnp.where(sublane > s, scaled[top], 0.0) * row
            for v in range(top + 1, count):
                tiles[v] = tiles[v] - scaled[v] * row
            if s == 7:
                tiles[top] = tiles[top] * lax.rsqrt(pivots)
    return tiles


def inverse_factor(matrix):
    n = matrix.shape[0]
    row = lax.broadcasted_iota(jnp.int32, (n, n), 0)
    lane = lax.broadcasted_iota(jnp.int32, (n, n), 1)
    tiles = [matrix[8 * v : 8 * v + 8] for v in range(n // 8)]
    per = BLOCK // 8
    for b in range(n // BLOCK):
        lo = BLOCK * b
        here = slice(per * b, per * b + per)
        tiles[here] = eliminate(tiles[here], lo)
        if lo + BLOCK < n:
            block = jnp.concatenate(tiles[here], axis=0)
            above = (lane[:BLOCK] > row[:BLOCK] + lo) & (lane[:BLOCK] < lo + BLOCK)
            update = dot_tn(block, jnp.where(above, 0.0, block))
            own = (lane[:8] >= lo) & (lane[:8] < lo + BLOCK)
            for v in range(per * b + per, n // 8):
                tiles[v] = jnp.where(own, 0.0, tiles[v]) - update[8 * v : 8 * v + 8]
    return jnp.where(lane <= row, jnp.concatenate(tiles, axis=0), 0.0)


def factor_body(own_ref, other_ref, probes_ref, high_ref, low_ref, basis_ref, coeffs_ref, basis_out, coeffs_out, sems):
    n = HALF
    k, pts = high_ref.shape
    own, other = (
        jnp.concatenate([ref[:, c].reshape(k, 128) for c in range(ref.shape[1])], axis=1)
        for ref in (own_ref, other_ref)
    )
    first = lax.axis_index("core") == 0
    moment = jnp.concatenate([jnp.where(first, own, other), jnp.where(first, other, own)], axis=1)
    probes = probes_ref[...]
    copies = []

    def write(held, ref, rows, cols, values):
        where = (pl.ds(rows, values.shape[0]), pl.ds(cols, values.shape[1]))
        held[where] = values
        copies.append(pltpu.make_async_copy(held.at[where], ref.at[where], sems.at[len(copies)]))
        copies[-1].start()

    upper = inverse_factor(dot_nt(moment[:n], probes[:n]))
    cross = dot_nn(upper, dot_nt(moment[:n], probes[n:]))
    rest = dot_nt(moment[n:], probes[n:]) - dot_tn(cross, cross)
    basis = dot_split(upper, high_ref[:n, :], low_ref[:n, :])
    write(basis_out, basis_ref, 0, 0, basis)
    coeffs = dot_split(upper, *split(moment[:n]))
    write(coeffs_out, coeffs_ref, 0, 0, coeffs)
    second = high_ref[n:, :].astype(jnp.float32) + low_ref[n:, :].astype(jnp.float32)
    high, low = split(second - dot_split(cross.T, *split(basis)))
    moment_high, moment_low = split(moment[n:] - dot_split(cross.T, *split(coeffs)))
    lower = inverse_factor(rest)
    for c in range(0, pts, pts // 2):
        cols = slice(c, c + pts // 2)
        write(basis_out, basis_ref, n, c, dot_split(lower, high[:, cols], low[:, cols]))
    write(coeffs_out, coeffs_ref, n, 0, dot_split(lower, moment_high, moment_low))
    for copy in copies:
        copy.wait()


def factor_and_apply(own, other, probes, high, low):
    k, pts = high.shape
    vmem = pl.BlockSpec(memory_space=pltpu.VMEM)
    return pl.pallas_call(
        factor_body,
        name="factor_and_apply",
        in_specs=[vmem] * 5,
        out_specs=[pl.BlockSpec(memory_space=pl.ANY), pl.BlockSpec(memory_space=pl.ANY)],
        out_shape=[
            jax.ShapeDtypeStruct((k, pts), jnp.float32),
            jax.ShapeDtypeStruct(probes.shape, jnp.float32),
        ],
        scratch_shapes=[
            pltpu.VMEM((k, pts), jnp.float32),
            pltpu.VMEM(probes.shape, jnp.float32),
            pltpu.SemaphoreType.DMA((5,)),
        ],
        compiler_params=pltpu.CompilerParams(vmem_limit_bytes=32 << 20),
    )(own, other, probes, high, low)


def on_device(fields, probes):
    chips = lax.axis_size("pts") * lax.axis_size("chip")
    devices = chips * lax.axis_size("core")
    per, n_points = fields.shape
    sent = fields.reshape(per, devices, n_points // devices).transpose(1, 0, 2)
    panels = lax.all_to_all(sent, AXES, split_axis=0, concat_axis=0, tiled=True)
    high, low, own, other = sketch(panels, probes, 1.0 / n_points)
    parts = (own + lax.ppermute(other, "core", SWAP)).reshape(chips, -1, 128)
    parts = lax.all_to_all(parts, CHIPS, split_axis=0, concat_axis=0, tiled=True)
    total = jnp.broadcast_to(jnp.sum(parts, axis=0)[None], parts.shape)
    total = lax.all_to_all(total, CHIPS, split_axis=0, concat_axis=0, tiled=True).reshape(own.shape)
    basis_rows, coeffs = factor_and_apply(total, lax.ppermute(total, "core", SWAP), probes, high, low)
    return (basis_rows, coeffs)


def solution(mesh):
    pts, hrs = mesh.devices.shape
    cores = Mesh(mesh.devices.reshape(pts, hrs // 2, 2), AXES)
    return jax.shard_map(
        on_device,
        mesh=cores,
        in_specs=(P(AXES, None), P()),
        out_specs=(P(None, AXES), P()),
        check_vma=False,
    )
```

```python
import jax
import jax.numpy as jnp
from jax import lax
from jax.experimental import pallas as pl
from jax.experimental.pallas import tpu as pltpu
from jax.sharding import Mesh
from jax.sharding import PartitionSpec as P

highest = lax.Precision.HIGHEST
CHIPS = ("pts", "chip")
AXES = ("pts", "chip", "core")
SWAP = ((0, 1), (1, 0))
CHUNK = 512
HALF = 128
BLOCK = 64
PANEL = 16
PIECES = 4


def dot_nn(left, right):
    return jnp.dot(left, right, precision=highest, preferred_element_type=jnp.float32)


def dot_tn(left, right):
    return lax.dot_general(
        left, right, (((0,), (0,)), ((), ())), precision=highest, preferred_element_type=jnp.float32
    )


def dot_nt(left, right):
    return lax.dot_general(
        left, right, (((1,), (1,)), ((), ())), precision=highest, preferred_element_type=jnp.float32
    )


def split(x):
    high = x.astype(jnp.bfloat16)
    return high, (x - high.astype(jnp.float32)).astype(jnp.bfloat16)


def dot_split(left, right_high, right_low):
    high, low = split(left)
    return jnp.dot(
        jnp.concatenate([high, high, low], axis=1),
        jnp.concatenate([right_high, right_low, right_high], axis=0),
        preferred_element_type=jnp.float32,
    )


def sketch_body(scale, panels_ref, probes_ref, high_ref, low_ref, own_ref, other_ref, fields_high, fields_low):
    devs, per, pts = panels_ref.shape
    hours = devs * per
    width = min(CHUNK, pts)
    probes = probes_ref[...]
    for c in range(pts // width):
        cols = slice(width * c, width * c + width)
        high, low = split(panels_ref[:, :, cols].reshape(hours, width))
        fields_high[:, cols] = high
        fields_low[:, cols] = low
        high_ref[:, cols], low_ref[:, cols] = split(dot_split(probes, high, low))
    high, low = high_ref[...], low_ref[...]
    moment = lax.dot_general(
        jnp.concatenate([high, high, low], axis=1),
        jnp.concatenate([fields_high[...], fields_low[...], fields_high[...]], axis=1),
        (((1,), (1,)), ((), ())),
        preferred_element_type=jnp.float32,
    )
    moment = (moment * scale).reshape(-1, 8, hours)
    first = lax.axis_index("core") == 0
    for c in range(hours // 256):
        left = moment[:, :, 128 * c : 128 * c + 128]
        right = moment[:, :, hours // 2 + 128 * c : hours // 2 + 128 * c + 128]
        own_ref[:, c] = jnp.where(first, left, right)
        other_ref[:, c] = jnp.where(first, right, left)


def sketch(panels, probes, scale):
    devs, per, pts = panels.shape
    k, hours = probes.shape
    vmem = pl.BlockSpec(memory_space=pltpu.VMEM)
    part = jax.ShapeDtypeStruct((k, pts), jnp.bfloat16)
    half = jax.ShapeDtypeStruct((k // 8, hours // 256, 8, 128), jnp.float32)
    return pl.pallas_call(
        lambda *refs: sketch_body(scale, *refs),
        name="sketch",
        in_specs=[vmem, vmem],
        out_specs=[vmem] * 4,
        out_shape=[part, part, half, half],
        scratch_shapes=[pltpu.VMEM((hours, pts), jnp.bfloat16), pltpu.VMEM((hours, pts), jnp.bfloat16)],
        compiler_params=pltpu.CompilerParams(vmem_limit_bytes=32 << 20),
    )(panels, probes)


def spread(x):
    return jnp.broadcast_to(x, (8, 128))


def eliminate(tiles, offset):
    sublane = lax.broadcasted_iota(jnp.int32, (8, 128), 0)
    lane = lax.broadcasted_iota(jnp.int32, (8, 128), 1)
    tiles = list(tiles)
    count = len(tiles)
    for t in range(0, count, PANEL // 8):
        first = offset + 8 * t
        own = (lane >= first) & (lane < first + PANEL)
        cols = {}
        for i in range(PANEL):
            for v in range(t + i // 8, count):
                cols[v, i] = spread(tiles[v][:, first + i : first + i + 1])
        for v in range(t, count):
            tiles[v] = jnp.where(own, jnp.where(lane - first - 8 * (v - t) == sublane, 1.0, 0.0), tiles[v])
        pivot = spread(cols[t, 0][0:1, :])
        for i in range(PANEL):
            top, s = t + i // 8, i % 8
            pivots = pivot if s == 0 else jnp.where(sublane == s, pivot, pivots)
            inverse = 1.0 / pivot
            scaled = {v: cols[v, i] * inverse for v in range(top, count)}
            if i + 1 < PANEL:
                u, r = t + (i + 1) // 8, (i + 1) % 8
                below = spread(cols[u, i][r : r + 1, :])
                pivot = spread(cols[u, i + 1][r : r + 1, :]) - (below * below) * inverse
            for j in range(i + 1, PANEL):
                u, r = t + j // 8, j % 8
                ratio = inverse * below if j == i + 1 else spread(scaled[u][r : r + 1, :])
                for v in range(u, count):
                    cols[v, j] = cols[v, j] - cols[v, i] * ratio
            row = spread(tiles[top][s : s + 1, :])
            if s < 7:
                tiles[top] = tiles[top] - jnp.where(sublane > s, scaled[top], 0.0) * row
            for v in range(top + 1, count):
                tiles[v] = tiles[v] - scaled[v] * row
            if s == 7:
                tiles[top] = tiles[top] * lax.rsqrt(pivots)
    return tiles


def inverse_factor(matrix):
    n = matrix.shape[0]
    row = lax.broadcasted_iota(jnp.int32, (n, n), 0)
    lane = lax.broadcasted_iota(jnp.int32, (n, n), 1)
    tiles = [matrix[8 * v : 8 * v + 8] for v in range(n // 8)]
    per = BLOCK // 8
    for b in range(n // BLOCK):
        lo = BLOCK * b
        here = slice(per * b, per * b + per)
        tiles[here] = eliminate(tiles[here], lo)
        if lo + BLOCK < n:
            block = jnp.concatenate(tiles[here], axis=0)
            above = (lane[:BLOCK] > row[:BLOCK] + lo) & (lane[:BLOCK] < lo + BLOCK)
            update = dot_tn(block, jnp.where(above, 0.0, block))
            own = (lane[:8] >= lo) & (lane[:8] < lo + BLOCK)
            for v in range(per * b + per, n // 8):
                tiles[v] = jnp.where(own, 0.0, tiles[v]) - update[8 * v : 8 * v + 8]
    return jnp.where(lane <= row, jnp.concatenate(tiles, axis=0), 0.0)


def factor_body(own_ref, other_ref, probes_ref, high_ref, low_ref, basis_ref, coeffs_ref, basis_out, coeffs_out, sems):
    n = HALF
    k, pts = high_ref.shape
    own, other = (
        jnp.concatenate([ref[:, c].reshape(k, 128) for c in range(ref.shape[1])], axis=1)
        for ref in (own_ref, other_ref)
    )
    first = lax.axis_index("core") == 0
    moment = jnp.concatenate([jnp.where(first, own, other), jnp.where(first, other, own)], axis=1)
    probes = probes_ref[...]
    copies = []

    def write(held, ref, rows, cols, values):
        where = (pl.ds(rows, values.shape[0]), pl.ds(cols, values.shape[1]))
        held[where] = values
        copies.append(pltpu.make_async_copy(held.at[where], ref.at[where], sems.at[len(copies)]))
        copies[-1].start()

    upper = inverse_factor(dot_nt(moment[:n], probes[:n]))
    cross = dot_nn(upper, dot_nt(moment[:n], probes[n:]))
    rest = dot_nt(moment[n:], probes[n:]) - dot_tn(cross, cross)
    basis = dot_split(upper, high_ref[:n, :], low_ref[:n, :])
    write(basis_out, basis_ref, 0, 0, basis)
    coeffs = dot_split(upper, *split(moment[:n]))
    write(coeffs_out, coeffs_ref, 0, 0, coeffs)
    second = high_ref[n:, :].astype(jnp.float32) + low_ref[n:, :].astype(jnp.float32)
    high, low = split(second - dot_split(cross.T, *split(basis)))
    moment_high, moment_low = split(moment[n:] - dot_split(cross.T, *split(coeffs)))
    lower = inverse_factor(rest)
    for c in range(0, pts, pts // PIECES):
        cols = slice(c, c + pts // PIECES)
        write(basis_out, basis_ref, n, c, dot_split(lower, high[:, cols], low[:, cols]))
    write(coeffs_out, coeffs_ref, n, 0, dot_split(lower, moment_high, moment_low))
    for copy in copies:
        copy.wait()


def factor_and_apply(own, other, probes, high, low):
    k, pts = high.shape
    vmem = pl.BlockSpec(memory_space=pltpu.VMEM)
    return pl.pallas_call(
        factor_body,
        name="factor_and_apply",
        in_specs=[vmem] * 5,
        out_specs=[pl.BlockSpec(memory_space=pl.ANY), pl.BlockSpec(memory_space=pl.ANY)],
        out_shape=[
            jax.ShapeDtypeStruct((k, pts), jnp.float32),
            jax.ShapeDtypeStruct(probes.shape, jnp.float32),
        ],
        scratch_shapes=[
            pltpu.VMEM((k, pts), jnp.float32),
            pltpu.VMEM(probes.shape, jnp.float32),
            pltpu.SemaphoreType.DMA((PIECES + 3,)),
        ],
        compiler_params=pltpu.CompilerParams(vmem_limit_bytes=32 << 20),
    )(own, other, probes, high, low)


def on_device(fields, probes):
    chips = lax.axis_size("pts") * lax.axis_size("chip")
    devices = chips * lax.axis_size("core")
    per, n_points = fields.shape
    sent = fields.reshape(per, devices, n_points // devices).transpose(1, 0, 2)
    panels = lax.all_to_all(sent, AXES, split_axis=0, concat_axis=0, tiled=True)
    high, low, own, other = sketch(panels, probes, 1.0 / n_points)
    parts = (own + lax.ppermute(other, "core", SWAP)).reshape(chips, -1, 128)
    parts = lax.all_to_all(parts, CHIPS, split_axis=0, concat_axis=0, tiled=True)
    total = jnp.broadcast_to(jnp.sum(parts, axis=0)[None], parts.shape)
    total = lax.all_to_all(total, CHIPS, split_axis=0, concat_axis=0, tiled=True).reshape(own.shape)
    basis_rows, coeffs = factor_and_apply(total, lax.ppermute(total, "core", SWAP), probes, high, low)
    return (basis_rows, coeffs)


def solution(mesh):
    pts, hrs = mesh.devices.shape
    cores = Mesh(mesh.devices.reshape(pts, hrs // 2, 2), AXES)
    return jax.shard_map(
        on_device,
        mesh=cores,
        in_specs=(P(AXES, None), P()),
        out_specs=(P(None, AXES), P()),
        check_vma=False,
    )
```

```python
import jax
import jax.numpy as jnp
from jax import lax
from jax.experimental import pallas as pl
from jax.experimental.pallas import tpu as pltpu
from jax.sharding import Mesh
from jax.sharding import PartitionSpec as P

highest = lax.Precision.HIGHEST
CHIPS = ("pts", "chip")
AXES = ("pts", "chip", "core")
SWAP = ((0, 1), (1, 0))
CHUNK = 512
HALF = 128
BLOCK = 64
PANEL = 16
PIECES = 4


def dot_nn(left, right):
    return jnp.dot(left, right, precision=highest, preferred_element_type=jnp.float32)


def dot_tn(left, right):
    return lax.dot_general(
        left, right, (((0,), (0,)), ((), ())), precision=highest, preferred_element_type=jnp.float32
    )


def dot_nt(left, right):
    return lax.dot_general(
        left, right, (((1,), (1,)), ((), ())), precision=highest, preferred_element_type=jnp.float32
    )


def split(x):
    high = x.astype(jnp.bfloat16)
    return high, (x - high.astype(jnp.float32)).astype(jnp.bfloat16)


def dot_split(left, right_high, right_low):
    high, low = split(left)
    return jnp.dot(
        jnp.concatenate([high, high, low], axis=1),
        jnp.concatenate([right_high, right_low, right_high], axis=0),
        preferred_element_type=jnp.float32,
    )


def sketch_body(scale, panels_ref, probes_ref, high_ref, low_ref, own_ref, other_ref, fields_high, fields_low):
    devs, per, pts = panels_ref.shape
    hours = devs * per
    width = min(CHUNK, pts)
    probes = probes_ref[...]
    for c in range(pts // width):
        cols = slice(width * c, width * c + width)
        high, low = split(panels_ref[:, :, cols].reshape(hours, width))
        fields_high[:, cols] = high
        fields_low[:, cols] = low
        high_ref[:, cols], low_ref[:, cols] = split(dot_split(probes, high, low))
    high, low = high_ref[...], low_ref[...]
    moment = lax.dot_general(
        jnp.concatenate([high, high, low], axis=1),
        jnp.concatenate([fields_high[...], fields_low[...], fields_high[...]], axis=1),
        (((1,), (1,)), ((), ())),
        preferred_element_type=jnp.float32,
    )
    moment = (moment * scale).reshape(-1, 8, hours)
    first = lax.axis_index("core") == 0
    for c in range(hours // 256):
        left = moment[:, :, 128 * c : 128 * c + 128]
        right = moment[:, :, hours // 2 + 128 * c : hours // 2 + 128 * c + 128]
        own_ref[:, c] = jnp.where(first, left, right)
        other_ref[:, c] = jnp.where(first, right, left)


def sketch(panels, probes, scale):
    devs, per, pts = panels.shape
    k, hours = probes.shape
    vmem = pl.BlockSpec(memory_space=pltpu.VMEM)
    part = jax.ShapeDtypeStruct((k, pts), jnp.bfloat16)
    half = jax.ShapeDtypeStruct((k // 8, hours // 256, 8, 128), jnp.float32)
    return pl.pallas_call(
        lambda *refs: sketch_body(scale, *refs),
        name="sketch",
        in_specs=[vmem, vmem],
        out_specs=[vmem] * 4,
        out_shape=[part, part, half, half],
        scratch_shapes=[pltpu.VMEM((hours, pts), jnp.bfloat16), pltpu.VMEM((hours, pts), jnp.bfloat16)],
        compiler_params=pltpu.CompilerParams(vmem_limit_bytes=32 << 20),
    )(panels, probes)


def spread(x):
    return jnp.broadcast_to(x, (8, 128))


def eliminate(tiles, offset):
    sublane = lax.broadcasted_iota(jnp.int32, (8, 128), 0)
    lane = lax.broadcasted_iota(jnp.int32, (8, 128), 1)
    tiles = list(tiles)
    count = len(tiles)
    for t in range(0, count, PANEL // 8):
        first = offset + 8 * t
        own = (lane >= first) & (lane < first + PANEL)
        cols = {}
        for i in range(PANEL):
            for v in range(t + i // 8, count):
                cols[v, i] = spread(tiles[v][:, first + i : first + i + 1])
        for v in range(t, count):
            tiles[v] = jnp.where(own, jnp.where(lane - first - 8 * (v - t) == sublane, 1.0, 0.0), tiles[v])
        pivot = spread(cols[t, 0][0:1, :])
        for i in range(PANEL):
            top, s = t + i // 8, i % 8
            pivots = pivot if s == 0 else jnp.where(sublane == s, pivot, pivots)
            inverse = 1.0 / pivot
            scaled = {v: cols[v, i] * inverse for v in range(top, count)}
            if i + 1 < PANEL:
                u, r = t + (i + 1) // 8, (i + 1) % 8
                below = spread(cols[u, i][r : r + 1, :])
                pivot = spread(cols[u, i + 1][r : r + 1, :]) - (below * below) * inverse
            for j in range(i + 1, PANEL):
                u, r = t + j // 8, j % 8
                ratio = inverse * below if j == i + 1 else spread(scaled[u][r : r + 1, :])
                for v in range(u, count):
                    cols[v, j] = cols[v, j] - cols[v, i] * ratio
            row = spread(tiles[top][s : s + 1, :])
            if s < 7:
                tiles[top] = tiles[top] - jnp.where(sublane > s, scaled[top], 0.0) * row
            for v in range(top + 1, count):
                tiles[v] = tiles[v] - scaled[v] * row
            if s == 7:
                tiles[top] = tiles[top] * lax.rsqrt(pivots)
    return tiles


def inverse_factor(matrix):
    n = matrix.shape[0]
    row = lax.broadcasted_iota(jnp.int32, (n, n), 0)
    lane = lax.broadcasted_iota(jnp.int32, (n, n), 1)
    tiles = [matrix[8 * v : 8 * v + 8] for v in range(n // 8)]
    per = BLOCK // 8
    for b in range(n // BLOCK):
        lo = BLOCK * b
        here = slice(per * b, per * b + per)
        tiles[here] = eliminate(tiles[here], lo)
        if lo + BLOCK < n:
            block = jnp.concatenate(tiles[here], axis=0)
            above = (lane[:BLOCK] > row[:BLOCK] + lo) & (lane[:BLOCK] < lo + BLOCK)
            update = dot_tn(block, jnp.where(above, 0.0, block))
            own = (lane[:8] >= lo) & (lane[:8] < lo + BLOCK)
            for v in range(per * b + per, n // 8):
                tiles[v] = jnp.where(own, 0.0, tiles[v]) - update[8 * v : 8 * v + 8]
    return jnp.where(lane <= row, jnp.concatenate(tiles, axis=0), 0.0)


def join(ref):
    return jnp.concatenate([ref[:, c].reshape(-1, 128) for c in range(ref.shape[1])], axis=1)


def gram_body(own_ref, probes_ref, gram_ref):
    half = probes_ref.shape[1] // 2
    first = lax.axis_index("core") == 0
    gram_ref[...] = dot_nt(join(own_ref), jnp.where(first, probes_ref[:, :half], probes_ref[:, half:]))


def own_gram(own, probes):
    k = probes.shape[0]
    vmem = pl.BlockSpec(memory_space=pltpu.VMEM)
    return pl.pallas_call(
        gram_body,
        name="own_gram",
        in_specs=[vmem, vmem],
        out_specs=vmem,
        out_shape=jax.ShapeDtypeStruct((k, k), jnp.float32),
        compiler_params=pltpu.CompilerParams(vmem_limit_bytes=32 << 20),
    )(own, probes)


def factor_body(gram_ref, own_ref, other_ref, probes_ref, high_ref, low_ref, basis_ref, coeffs_ref, basis_out, coeffs_out, sems):
    n = HALF
    k, pts = high_ref.shape
    own, other = join(own_ref), join(other_ref)
    first = lax.axis_index("core") == 0
    moment = jnp.concatenate([jnp.where(first, own, other), jnp.where(first, other, own)], axis=1)
    half = probes_ref.shape[1] // 2
    probes = jnp.where(first, probes_ref[:, half:], probes_ref[:, :half])
    copies = []

    def write(held, ref, rows, cols, values):
        where = (pl.ds(rows, values.shape[0]), pl.ds(cols, values.shape[1]))
        held[where] = values
        copies.append(pltpu.make_async_copy(held.at[where], ref.at[where], sems.at[len(copies)]))
        copies[-1].start()

    upper = inverse_factor(gram_ref[:n, :n] + dot_nt(other[:n], probes[:n]))
    cross = dot_nn(upper, gram_ref[:n, n:] + dot_nt(other[:n], probes[n:]))
    rest = gram_ref[n:, n:] + dot_nt(other[n:], probes[n:]) - dot_tn(cross, cross)
    basis = dot_split(upper, high_ref[:n, :], low_ref[:n, :])
    write(basis_out, basis_ref, 0, 0, basis)
    coeffs = dot_split(upper, *split(moment[:n]))
    write(coeffs_out, coeffs_ref, 0, 0, coeffs)
    second = high_ref[n:, :].astype(jnp.float32) + low_ref[n:, :].astype(jnp.float32)
    high, low = split(second - dot_split(cross.T, *split(basis)))
    moment_high, moment_low = split(moment[n:] - dot_split(cross.T, *split(coeffs)))
    lower = inverse_factor(rest)
    for c in range(0, pts, pts // PIECES):
        cols = slice(c, c + pts // PIECES)
        write(basis_out, basis_ref, n, c, dot_split(lower, high[:, cols], low[:, cols]))
    write(coeffs_out, coeffs_ref, n, 0, dot_split(lower, moment_high, moment_low))
    for copy in copies:
        copy.wait()


def factor_and_apply(gram, own, other, probes, high, low):
    k, pts = high.shape
    vmem = pl.BlockSpec(memory_space=pltpu.VMEM)
    return pl.pallas_call(
        factor_body,
        name="factor_and_apply",
        in_specs=[vmem] * 6,
        out_specs=[pl.BlockSpec(memory_space=pl.ANY), pl.BlockSpec(memory_space=pl.ANY)],
        out_shape=[
            jax.ShapeDtypeStruct((k, pts), jnp.float32),
            jax.ShapeDtypeStruct(probes.shape, jnp.float32),
        ],
        scratch_shapes=[
            pltpu.VMEM((k, pts), jnp.float32),
            pltpu.VMEM(probes.shape, jnp.float32),
            pltpu.SemaphoreType.DMA((PIECES + 3,)),
        ],
        compiler_params=pltpu.CompilerParams(vmem_limit_bytes=32 << 20),
    )(gram, own, other, probes, high, low)


def on_device(fields, probes):
    chips = lax.axis_size("pts") * lax.axis_size("chip")
    devices = chips * lax.axis_size("core")
    per, n_points = fields.shape
    sent = fields.reshape(per, devices, n_points // devices).transpose(1, 0, 2)
    panels = lax.all_to_all(sent, AXES, split_axis=0, concat_axis=0, tiled=True)
    high, low, own, other = sketch(panels, probes, 1.0 / n_points)
    parts = (own + lax.ppermute(other, "core", SWAP)).reshape(chips, -1, 128)
    parts = lax.all_to_all(parts, CHIPS, split_axis=0, concat_axis=0, tiled=True)
    total = jnp.broadcast_to(jnp.sum(parts, axis=0)[None], parts.shape)
    total = lax.all_to_all(total, CHIPS, split_axis=0, concat_axis=0, tiled=True).reshape(own.shape)
    swapped = lax.ppermute(total, "core", SWAP)
    basis_rows, coeffs = factor_and_apply(own_gram(total, probes), total, swapped, probes, high, low)
    return (basis_rows, coeffs)


def solution(mesh):
    pts, hrs = mesh.devices.shape
    cores = Mesh(mesh.devices.reshape(pts, hrs // 2, 2), AXES)
    return jax.shard_map(
        on_device,
        mesh=cores,
        in_specs=(P(AXES, None), P()),
        out_specs=(P(None, AXES), P()),
        check_vma=False,
    )
```

```python
import jax
import jax.numpy as jnp
from jax import lax
from jax.experimental import pallas as pl
from jax.experimental.pallas import tpu as pltpu
from jax.sharding import Mesh
from jax.sharding import PartitionSpec as P

highest = lax.Precision.HIGHEST
CHIPS = ("pts", "chip")
AXES = ("pts", "chip", "core")
SWAP = ((0, 1), (1, 0))
CHUNK = 512
HALF = 128
BLOCK = 64
PANEL = 16
PIECES = 4


def dot_nn(left, right):
    return jnp.dot(left, right, precision=highest, preferred_element_type=jnp.float32)


def dot_tn(left, right):
    return lax.dot_general(
        left, right, (((0,), (0,)), ((), ())), precision=highest, preferred_element_type=jnp.float32
    )


def dot_nt(left, right):
    return lax.dot_general(
        left, right, (((1,), (1,)), ((), ())), precision=highest, preferred_element_type=jnp.float32
    )


def split(x):
    high = x.astype(jnp.bfloat16)
    return high, (x - high.astype(jnp.float32)).astype(jnp.bfloat16)


def dot_split(left, right_high, right_low):
    high, low = split(left)
    return jnp.dot(
        jnp.concatenate([high, high, low], axis=1),
        jnp.concatenate([right_high, right_low, right_high], axis=0),
        preferred_element_type=jnp.float32,
    )


def sketch_body(scale, panels_ref, probes_ref, high_ref, low_ref, own_ref, other_ref, fields_high, fields_low):
    devs, per, pts = panels_ref.shape
    hours = devs * per
    width = min(CHUNK, pts)
    probes = probes_ref[...]
    for c in range(pts // width):
        cols = slice(width * c, width * c + width)
        high, low = split(panels_ref[:, :, cols].reshape(hours, width))
        fields_high[:, cols] = high
        fields_low[:, cols] = low
        high_ref[:, cols], low_ref[:, cols] = split(dot_split(probes, high, low))
    high, low = high_ref[...], low_ref[...]
    moment = lax.dot_general(
        jnp.concatenate([high, high, low], axis=1),
        jnp.concatenate([fields_high[...], fields_low[...], fields_high[...]], axis=1),
        (((1,), (1,)), ((), ())),
        preferred_element_type=jnp.float32,
    )
    moment = (moment * scale).reshape(-1, 8, hours)
    first = lax.axis_index("core") == 0
    for c in range(hours // 256):
        left = moment[:, :, 128 * c : 128 * c + 128]
        right = moment[:, :, hours // 2 + 128 * c : hours // 2 + 128 * c + 128]
        own_ref[:, c] = jnp.where(first, left, right)
        other_ref[:, c] = jnp.where(first, right, left)


def sketch(panels, probes, scale):
    devs, per, pts = panels.shape
    k, hours = probes.shape
    vmem = pl.BlockSpec(memory_space=pltpu.VMEM)
    part = jax.ShapeDtypeStruct((k, pts), jnp.bfloat16)
    half = jax.ShapeDtypeStruct((k // 8, hours // 256, 8, 128), jnp.float32)
    return pl.pallas_call(
        lambda *refs: sketch_body(scale, *refs),
        name="sketch",
        in_specs=[vmem, vmem],
        out_specs=[vmem] * 4,
        out_shape=[part, part, half, half],
        scratch_shapes=[pltpu.VMEM((hours, pts), jnp.bfloat16), pltpu.VMEM((hours, pts), jnp.bfloat16)],
        compiler_params=pltpu.CompilerParams(vmem_limit_bytes=32 << 20),
    )(panels, probes)


def spread(x):
    return jnp.broadcast_to(x, (8, 128))


def eliminate(tiles, offset):
    sublane = lax.broadcasted_iota(jnp.int32, (8, 128), 0)
    lane = lax.broadcasted_iota(jnp.int32, (8, 128), 1)
    tiles = list(tiles)
    count = len(tiles)
    for t in range(0, count, PANEL // 8):
        first = offset + 8 * t
        own = (lane >= first) & (lane < first + PANEL)
        cols = {}
        for i in range(PANEL):
            for v in range(t + i // 8, count):
                cols[v, i] = spread(tiles[v][:, first + i : first + i + 1])
        for v in range(t, count):
            tiles[v] = jnp.where(own, jnp.where(lane - first - 8 * (v - t) == sublane, 1.0, 0.0), tiles[v])
        pivot = spread(cols[t, 0][0:1, :])
        for i in range(PANEL):
            top, s = t + i // 8, i % 8
            pivots = pivot if s == 0 else jnp.where(sublane == s, pivot, pivots)
            inverse = 1.0 / pivot
            scaled = {v: cols[v, i] * inverse for v in range(top, count)}
            if i + 1 < PANEL:
                u, r = t + (i + 1) // 8, (i + 1) % 8
                below = spread(cols[u, i][r : r + 1, :])
                pivot = spread(cols[u, i + 1][r : r + 1, :]) - (below * below) * inverse
            for j in range(i + 1, PANEL):
                u, r = t + j // 8, j % 8
                ratio = inverse * below if j == i + 1 else spread(scaled[u][r : r + 1, :])
                for v in range(u, count):
                    cols[v, j] = cols[v, j] - cols[v, i] * ratio
            row = spread(tiles[top][s : s + 1, :])
            if s < 7:
                tiles[top] = tiles[top] - jnp.where(sublane > s, scaled[top], 0.0) * row
            for v in range(top + 1, count):
                tiles[v] = tiles[v] - scaled[v] * row
            if s == 7:
                tiles[top] = tiles[top] * lax.rsqrt(pivots)
    return tiles


def inverse_factor(matrix):
    n = matrix.shape[0]
    row = lax.broadcasted_iota(jnp.int32, (n, n), 0)
    lane = lax.broadcasted_iota(jnp.int32, (n, n), 1)
    tiles = [matrix[8 * v : 8 * v + 8] for v in range(n // 8)]
    per = BLOCK // 8
    for b in range(n // BLOCK):
        lo = BLOCK * b
        here = slice(per * b, per * b + per)
        tiles[here] = eliminate(tiles[here], lo)
        if lo + BLOCK < n:
            block = jnp.concatenate(tiles[here], axis=0)
            above = (lane[:BLOCK] > row[:BLOCK] + lo) & (lane[:BLOCK] < lo + BLOCK)
            update = dot_tn(block, jnp.where(above, 0.0, block))
            own = (lane[:8] >= lo) & (lane[:8] < lo + BLOCK)
            for v in range(per * b + per, n // 8):
                tiles[v] = jnp.where(own, 0.0, tiles[v]) - update[8 * v : 8 * v + 8]
    return jnp.where(lane <= row, jnp.concatenate(tiles, axis=0), 0.0)


def join(ref):
    return jnp.concatenate([ref[:, c].reshape(-1, 128) for c in range(ref.shape[1])], axis=1)


def gram_body(own_ref, probes_ref, gram_ref):
    half = probes_ref.shape[1] // 2
    first = lax.axis_index("core") == 0
    gram_ref[...] = dot_nt(join(own_ref), jnp.where(first, probes_ref[:, :half], probes_ref[:, half:]))


def own_gram(own, probes):
    k = probes.shape[0]
    vmem = pl.BlockSpec(memory_space=pltpu.VMEM)
    return pl.pallas_call(
        gram_body,
        name="own_gram",
        in_specs=[vmem, vmem],
        out_specs=vmem,
        out_shape=jax.ShapeDtypeStruct((k, k), jnp.float32),
        compiler_params=pltpu.CompilerParams(vmem_limit_bytes=32 << 20),
    )(own, probes)


def merge_body(high_ref, low_ref, whole_ref):
    whole_ref[...] = high_ref[HALF:, :].astype(jnp.float32) + low_ref[HALF:, :].astype(jnp.float32)


def merge_second(high, low):
    k, pts = high.shape
    vmem = pl.BlockSpec(memory_space=pltpu.VMEM)
    return pl.pallas_call(
        merge_body,
        name="merge_second",
        in_specs=[vmem, vmem],
        out_specs=vmem,
        out_shape=jax.ShapeDtypeStruct((k - HALF, pts), jnp.float32),
        compiler_params=pltpu.CompilerParams(vmem_limit_bytes=32 << 20),
    )(high, low)


def factor_body(gram_ref, own_ref, other_ref, probes_ref, high_ref, low_ref, second_ref, basis_ref, coeffs_ref, basis_out, coeffs_out, sems):
    n = HALF
    k, pts = high_ref.shape
    own, other = join(own_ref), join(other_ref)
    first = lax.axis_index("core") == 0
    moment = jnp.concatenate([jnp.where(first, own, other), jnp.where(first, other, own)], axis=1)
    half = probes_ref.shape[1] // 2
    probes = jnp.where(first, probes_ref[:, half:], probes_ref[:, :half])
    copies = []

    def write(held, ref, rows, cols, values):
        where = (pl.ds(rows, values.shape[0]), pl.ds(cols, values.shape[1]))
        held[where] = values
        copies.append(pltpu.make_async_copy(held.at[where], ref.at[where], sems.at[len(copies)]))
        copies[-1].start()

    upper = inverse_factor(gram_ref[:n, :n] + dot_nt(other[:n], probes[:n]))
    cross = dot_nn(upper, gram_ref[:n, n:] + dot_nt(other[:n], probes[n:]))
    rest = gram_ref[n:, n:] + dot_nt(other[n:], probes[n:]) - dot_tn(cross, cross)
    basis = dot_split(upper, high_ref[:n, :], low_ref[:n, :])
    write(basis_out, basis_ref, 0, 0, basis)
    coeffs = dot_split(upper, *split(moment[:n]))
    write(coeffs_out, coeffs_ref, 0, 0, coeffs)
    high, low = split(second_ref[...] - dot_split(cross.T, *split(basis)))
    moment_high, moment_low = split(moment[n:] - dot_split(cross.T, *split(coeffs)))
    lower = inverse_factor(rest)
    for c in range(0, pts, pts // PIECES):
        cols = slice(c, c + pts // PIECES)
        write(basis_out, basis_ref, n, c, dot_split(lower, high[:, cols], low[:, cols]))
    write(coeffs_out, coeffs_ref, n, 0, dot_split(lower, moment_high, moment_low))
    for copy in copies:
        copy.wait()


def factor_and_apply(gram, own, other, probes, high, low, second):
    k, pts = high.shape
    vmem = pl.BlockSpec(memory_space=pltpu.VMEM)
    return pl.pallas_call(
        factor_body,
        name="factor_and_apply",
        in_specs=[vmem] * 7,
        out_specs=[pl.BlockSpec(memory_space=pl.ANY), pl.BlockSpec(memory_space=pl.ANY)],
        out_shape=[
            jax.ShapeDtypeStruct((k, pts), jnp.float32),
            jax.ShapeDtypeStruct(probes.shape, jnp.float32),
        ],
        scratch_shapes=[
            pltpu.VMEM((k, pts), jnp.float32),
            pltpu.VMEM(probes.shape, jnp.float32),
            pltpu.SemaphoreType.DMA((PIECES + 3,)),
        ],
        compiler_params=pltpu.CompilerParams(vmem_limit_bytes=32 << 20),
    )(gram, own, other, probes, high, low, second)


def on_device(fields, probes):
    chips = lax.axis_size("pts") * lax.axis_size("chip")
    devices = chips * lax.axis_size("core")
    per, n_points = fields.shape
    sent = fields.reshape(per, devices, n_points // devices).transpose(1, 0, 2)
    panels = lax.all_to_all(sent, AXES, split_axis=0, concat_axis=0, tiled=True)
    high, low, own, other = sketch(panels, probes, 1.0 / n_points)
    second = merge_second(high, low)
    parts = (own + lax.ppermute(other, "core", SWAP)).reshape(chips, -1, 128)
    parts = lax.all_to_all(parts, CHIPS, split_axis=0, concat_axis=0, tiled=True)
    total = jnp.broadcast_to(jnp.sum(parts, axis=0)[None], parts.shape)
    total = lax.all_to_all(total, CHIPS, split_axis=0, concat_axis=0, tiled=True).reshape(own.shape)
    swapped = lax.ppermute(total, "core", SWAP)
    basis_rows, coeffs = factor_and_apply(own_gram(total, probes), total, swapped, probes, high, low, second)
    return (basis_rows, coeffs)


def solution(mesh):
    pts, hrs = mesh.devices.shape
    cores = Mesh(mesh.devices.reshape(pts, hrs // 2, 2), AXES)
    return jax.shard_map(
        on_device,
        mesh=cores,
        in_specs=(P(AXES, None), P()),
        out_specs=(P(None, AXES), P()),
        check_vma=False,
    )
```
